768 devices in a mesh: dp: 24 (over y, z_hi), ctx: 32 (over z_lo, x, core).
Axes of the slice: x: 4, y: 8, z: 12 (z_hi: 3, z_lo: 4; z = z_hi * 4 + z_lo), core: 2. Of those that a mesh axis runs over, the one named last changes fastest.
Arguments:
- query_raw: bfloat16 [24, 4096, 2560], P('dp', 'ctx'), may hold values from -6 to 6
- key_raw: bfloat16 [24, 4096, 2560], P('dp', 'ctx'), may hold values from -6 to 6
- value_rows: bfloat16 [24, 4096, 2560], P('dp', 'ctx'), may hold values from -6 to 6
- out_grad: bfloat16 [24, 4096, 2560], P('dp', 'ctx'), may hold values from -6 to 6
- query_gain: float32 [2560], replicated, may hold values from 0.1 to 1.9
- key_gain: float32 [2560], replicated, may hold values from 0.1 to 1.9
Outputs:
- query_grad: bfloat16 [24, 4096, 2560], P('dp', 'ctx')
- key_grad: bfloat16 [24, 4096, 2560], P('dp', 'ctx')
- value_grad: bfloat16 [24, 4096, 2560], P('dp', 'ctx')
- gain_grads: float32 [2, 2560], replicated
The draws below stay inside these ranges and needn't reach their ends.
All inputs are finite; a program needn't handle non-finite values.
Results may differ from the reference program's by a relative error of at most 0.011.
Values may be sent and summed in bfloat16 or wider, within the bound.
A program may use at most 32 MiB of HBM per device.

```python
import jax
import jax.numpy as jnp
from jax import lax

HEADS = 20
HEAD_DIM = 128
TILE = 128
MARGIN = 32
FEAT = 2560
NT = 32
TOKENS = 4096
CLIPS = 24


def draw_query_raw(key, part):
    shape_all = (CLIPS, TOKENS, FEAT)
    noise_key = jax.random.fold_in(key, 1)
    return jnp.clip(jax.random.normal(noise_key, shape_all, jnp.float32), -6.0, 6.0).astype(jnp.bfloat16)


def draw_key_raw(key, part):
    shape_all = (CLIPS, TOKENS, FEAT)
    noise_key = jax.random.fold_in(key, 2)
    return jnp.clip(jax.random.normal(noise_key, shape_all, jnp.float32), -6.0, 6.0).astype(jnp.bfloat16)


def block_levels(own_key, extent, cuts, smallest, top_value):
    gain = 1.0
    for axis_at, shards_of in cuts:
        draws = jax.random.uniform(jax.random.fold_in(jax.random.fold_in(own_key, 6), axis_at), (shards_of,), jnp.float32, smallest / len(cuts), top_value / len(cuts))
        gain = gain * jnp.repeat(jnp.exp(draws), extent[axis_at] // shards_of).reshape((-1,) + (1,) * (len(extent) - 1 - axis_at))
    return gain


def noise(own_key, shape, deviation, most, cuts=(), kind=jnp.bfloat16):
    array = jax.random.normal(own_key, shape, jnp.float32) * deviation
    if len(cuts) > 0:
        array = block_levels(own_key, shape, cuts, -0.22, 0.18) * array
    return jnp.clip(array, min=-most, max=most).astype(kind)


def setup_inputs(seed: int = 0) -> dict:
    keys = jax.random.split(jax.random.key(seed), 7)
    return {
        "query_raw": draw_query_raw(jax.random.fold_in(keys[6], 71), 0),
        "key_raw": draw_key_raw(jax.random.fold_in(keys[6], 71), 0),
        "value_rows": noise(keys[2], (CLIPS, TOKENS, FEAT), 1.0, 6.0, ((0, 24), (1, 32))),
        "out_grad": noise(keys[3], (CLIPS, TOKENS, FEAT), 1.0, 6.0, ((0, 24), (1, 32))),
        "query_gain": jnp.clip(1.0 + 0.18 * jax.random.normal(keys[4], (FEAT,), jnp.float32), 0.1, 1.9),
        "key_gain": jnp.clip(1.0 + 0.18 * jax.random.normal(keys[5], (FEAT,), jnp.float32), 0.1, 1.9),
    }


NORM_EPS = 1e-06

def normalize(raw_rows, gain_row):
    widened = raw_rows.astype(jnp.float32)
    factor = lax.rsqrt(lax.optimization_barrier(jnp.mean(widened * widened, axis=-1, keepdims=True)) + NORM_EPS)
    return ((widened * factor * gain_row).astype(jnp.bfloat16), factor)

def norm_backward(raw_rows, factor, gain_row, upstream):
    widened = raw_rows.astype(jnp.float32)
    scaled = upstream * gain_row
    inner = lax.optimization_barrier(jnp.mean(widened * scaled, axis=-1, keepdims=True))
    raw_grad = factor * scaled - widened * (factor * factor * factor) * inner
    gain_part = lax.optimization_barrier(jnp.sum(upstream * widened * factor, axis=0))
    return (raw_grad.astype(jnp.bfloat16), gain_part)

def rounded(values):
    return lax.optimization_barrier(values.astype(jnp.bfloat16)).astype(jnp.float32)

def tile_pass(query_rows, key_rows, value_rows, grad_rows, valid_keys):
    tile_rows = query_rows.shape[0]
    window_rows = key_rows.shape[0]
    score_scale = HEAD_DIM ** (-0.5)
    query_heads = query_rows.astype(jnp.float32).reshape(tile_rows, HEADS, HEAD_DIM)
    key_heads = key_rows.astype(jnp.float32).reshape(window_rows, HEADS, HEAD_DIM)
    value_heads = value_rows.astype(jnp.float32).reshape(window_rows, HEADS, HEAD_DIM)
    grad_heads = grad_rows.astype(jnp.float32).reshape(tile_rows, HEADS, HEAD_DIM)
    scores = jnp.einsum('qhd,khd->hqk', query_heads, key_heads) * score_scale
    scores = jnp.where(valid_keys[None, None, :], scores, -1e+30)
    row_max = lax.optimization_barrier(jnp.max(scores, axis=-1, keepdims=True))
    exponents = jnp.exp(scores - row_max)
    attn_probs = exponents / lax.optimization_barrier(jnp.sum(exponents, axis=-1, keepdims=True))
    probs_half = rounded(attn_probs)
    attn_out = jnp.einsum('hqk,khd->qhd', probs_half, value_heads)
    row_delta = lax.optimization_barrier(jnp.sum(grad_heads * attn_out, axis=-1))
    grad_probs = jnp.einsum('qhd,khd->hqk', grad_heads, value_heads)
    grad_scores = rounded(attn_probs * (grad_probs - jnp.transpose(row_delta)[:, :, None]))
    query_grad = (jnp.einsum('hqk,khd->qhd', grad_scores, key_heads) * score_scale).reshape(tile_rows, HEADS * HEAD_DIM)
    key_terms = (jnp.einsum('hqk,qhd->khd', grad_scores, query_heads) * score_scale).astype(jnp.bfloat16)
    value_terms = jnp.einsum('hqk,qhd->khd', probs_half, grad_heads).astype(jnp.bfloat16)
    return (query_grad, key_terms.reshape(window_rows, HEADS * HEAD_DIM), value_terms.reshape(window_rows, HEADS * HEAD_DIM))

def window_tiles(tiles):
    blank = jnp.zeros((1, TILE, FEAT), tiles.dtype)
    padded = jnp.concatenate([blank, tiles, blank], axis=0)
    return jnp.concatenate([padded[:-2, TILE - MARGIN:], padded[1:-1], padded[2:, :MARGIN]], axis=1)

def collect(terms):
    widened = terms.astype(jnp.float32)
    blank = jnp.zeros((1, MARGIN, FEAT), jnp.float32)
    from_upper = jnp.concatenate([widened[1:, :MARGIN], blank], axis=0)
    from_lower = jnp.concatenate([blank, widened[:-1, MARGIN + TILE:]], axis=0)
    middle_zero = jnp.zeros((NT, TILE - MARGIN, FEAT), jnp.float32)
    upper_full = jnp.concatenate([middle_zero, from_upper], axis=1)
    lower_full = jnp.concatenate([from_lower, middle_zero], axis=1)
    return widened[:, MARGIN:MARGIN + TILE] + upper_full + lower_full

def reference(query_raw, key_raw, value_rows, out_grad, query_gain, key_gain):
    tile_ids = jnp.arange(NT, dtype=jnp.int32)[:, None]
    slot_ids = jnp.arange(TILE + 2 * MARGIN, dtype=jnp.int32)[None, :]
    valid = jnp.logical_not((slot_ids < MARGIN) & (tile_ids == 0) | (slot_ids >= MARGIN + TILE) & (tile_ids == NT - 1))

    def per_clip(operands):
        q_clip, k_clip, v_clip, g_clip = operands
        query_norm, query_factor = normalize(q_clip, query_gain)
        key_norm, key_factor = normalize(k_clip, key_gain)
        query_tiles = query_norm.reshape(NT, TILE, FEAT)
        window_keys = window_tiles(key_norm.reshape(NT, TILE, FEAT))
        window_values = window_tiles(v_clip.reshape(NT, TILE, FEAT))
        grad_tiles = g_clip.reshape(NT, TILE, FEAT)
        query_grad, key_terms, value_terms = jax.vmap(tile_pass)(query_tiles, window_keys, window_values, grad_tiles, valid)
        key_sum = collect(key_terms)
        value_sum = collect(value_terms)
        query_raw_grad, query_gain_part = norm_backward(q_clip, query_factor, query_gain, query_grad.reshape(TOKENS, FEAT))
        key_raw_grad, key_gain_part = norm_backward(k_clip, key_factor, key_gain, key_sum.reshape(TOKENS, FEAT))
        return (query_raw_grad, key_raw_grad, value_sum.reshape(TOKENS, FEAT).astype(jnp.bfloat16), query_gain_part, key_gain_part)
    results = lax.map(per_clip, (query_raw, key_raw, value_rows, out_grad))
    gain_grads = jnp.stack([lax.optimization_barrier(jnp.sum(results[3], axis=0)), lax.optimization_barrier(jnp.sum(results[4], axis=0))])
    return (results[0], results[1], results[2], gain_grads)
```

```python
import jax
import jax.numpy as jnp
from jax import lax
from jax.sharding import PartitionSpec as P

HEADS = 20
HEAD_DIM = 128


NORM_EPS = 1e-06


def padded(block, sides, width):
    for axis, dim in sides:
        count = lax.axis_size(axis)
        forward = [(i, i + 1) for i in range(count - 1)]
        backward = [(target, source) for source, target in forward]
        low = lax.ppermute(
            lax.slice_in_dim(block, block.shape[dim] - width, None, axis=dim), axis, forward
        )
        high = lax.ppermute(lax.slice_in_dim(block, 0, width, axis=dim), axis, backward)
        block = jnp.concatenate([low, block, high], axis=dim)
    return block


AXIS_PARTS = {"ctx": (4, 4, 2), "dp": (8, 3)}


def part_steps(axis):
    total = lax.axis_size(axis)
    sizes = AXIS_PARTS[axis]
    stride = total
    steps = []
    for size in sizes:
        stride //= size
        steps.append((size, stride))
    return total, steps


def partner_pairs(total, size, stride, move):
    pairs = []
    for i in range(total):
        c = (i // stride) % size
        pairs.append((i, i + (move(c) - c) * stride))
    return pairs


def axis_sum(x, axis):
    total, steps = part_steps(axis)
    for size, stride in reversed(steps):
        if size & (size - 1):
            acc = x
            for k in range(1, size):
                acc = acc + lax.ppermute(
                    x, axis, partner_pairs(total, size, stride, lambda c: (c + k) % size)
                )
            x = acc
        else:
            d = 1
            while d < size:
                x = x + lax.ppermute(
                    x, axis, partner_pairs(total, size, stride, lambda c: c ^ d)
                )
                d *= 2
    return x


def mesh_sum(x):
    return axis_sum(axis_sum(x, "dp"), "ctx")


def shifted(block, axis, distance):
    devices = range(lax.axis_size(axis))
    route = [(i - distance, i) for i in devices if i - distance in devices]
    return lax.ppermute(block, axis, route)


def normalize(raw_rows, gain_row):
    widened = raw_rows.astype(jnp.float32)
    factor = lax.rsqrt(jnp.mean(widened * widened, axis=-1, keepdims=True) + NORM_EPS)
    return ((widened * factor * gain_row).astype(jnp.bfloat16), factor)


def norm_backward(raw_rows, factor, gain_row, upstream):
    widened = raw_rows.astype(jnp.float32)
    scaled = upstream * gain_row
    inner = jnp.mean(widened * scaled, axis=-1, keepdims=True)
    raw_grad = factor * scaled - widened * (factor * factor * factor) * inner
    gain_part = jnp.sum(upstream * widened * factor, axis=0)
    return (raw_grad.astype(jnp.bfloat16), gain_part)


def split_heads(matrix):
    return matrix.reshape(matrix.shape[0], HEADS, HEAD_DIM)


def tile_pass(query_rows, key_rows, value_rows, grad_rows, valid_keys):
    score_scale = HEAD_DIM ** (-0.5)
    query_heads = split_heads(query_rows)
    key_heads = split_heads(key_rows)
    value_heads = split_heads(value_rows)
    grad_heads = split_heads(grad_rows)
    scores = (
        jnp.einsum("qhd,khd->hqk", query_heads, key_heads, preferred_element_type=jnp.float32)
        * score_scale
    )
    scores = jnp.where(valid_keys[None, None, :], scores, -1e30)
    row_max = jnp.max(scores, axis=-1, keepdims=True)
    exponents = jnp.exp(scores - row_max)
    row_sum = jnp.sum(exponents, axis=-1, keepdims=True)
    attn_probs = exponents / row_sum
    probs_half = attn_probs.astype(jnp.bfloat16)
    attn_out = jnp.einsum(
        "hqk,khd->qhd", probs_half, value_heads, preferred_element_type=jnp.float32
    )
    row_delta = jnp.sum(grad_heads.astype(jnp.float32) * attn_out, axis=-1)
    grad_probs = jnp.einsum(
        "qhd,khd->hqk", grad_heads, value_heads, preferred_element_type=jnp.float32
    )
    grad_scores = (attn_probs * (grad_probs - jnp.transpose(row_delta)[:, :, None])).astype(
        jnp.bfloat16
    )
    query_grad = (
        jnp.einsum("hqk,khd->qhd", grad_scores, key_heads, preferred_element_type=jnp.float32)
        * score_scale
    )
    key_terms = (
        jnp.einsum("hqk,qhd->khd", grad_scores, query_heads, preferred_element_type=jnp.float32)
        * score_scale
    ).astype(jnp.bfloat16)
    value_terms = jnp.einsum(
        "hqk,qhd->khd", probs_half, grad_heads, preferred_element_type=jnp.float32
    ).astype(jnp.bfloat16)
    log_total = jnp.transpose((row_max + jnp.log(row_sum))[:, :, 0])
    flat_width = HEADS * HEAD_DIM
    return (
        query_grad.reshape(query_rows.shape[0], flat_width),
        key_terms.reshape(key_rows.shape[0], flat_width),
        value_terms.reshape(key_rows.shape[0], flat_width),
        log_total,
        row_delta,
    )


def per_device(query_raw, key_raw, value_rows, out_grad, query_gain, key_gain):
    tile_rows = query_raw.shape[1]
    margin = tile_rows // 4
    ctx_count = lax.axis_size("ctx")
    position = lax.axis_index("ctx")
    query_norm, query_factor = normalize(query_raw[0], query_gain)
    key_norm, key_factor = normalize(key_raw[0], key_gain)
    own_values = value_rows[0]
    own_grads = out_grad[0]
    key_window = padded(jnp.stack([key_norm, own_values]), (("ctx", 1),), margin)
    slot_ids = jnp.arange(tile_rows + 2 * margin, dtype=jnp.int32)
    valid_keys = jnp.logical_not(
        (slot_ids < margin) & (position == 0)
        | (slot_ids >= margin + tile_rows) & (position == ctx_count - 1)
    )
    query_grad, key_terms, value_terms, log_total, row_delta = tile_pass(
        query_norm, key_window[0], key_window[1], own_grads, valid_keys
    )
    key_sum = key_terms[margin : margin + tile_rows].astype(jnp.float32)
    value_sum = value_terms[margin : margin + tile_rows].astype(jnp.float32)
    edge_pad = ((0, tile_rows - margin), (0, 0))
    tail_pad = ((tile_rows - margin, 0), (0, 0))
    upper_slot = jnp.stack([key_terms[margin + tile_rows :], value_terms[margin + tile_rows :]])
    lower_slot = jnp.stack([key_terms[:margin], value_terms[:margin]])
    from_lower = shifted(upper_slot, "ctx", 1)
    from_upper = shifted(lower_slot, "ctx", -1)
    key_sum = (
        key_sum
        + jnp.pad(from_lower[0].astype(jnp.float32), edge_pad)
        + jnp.pad(from_upper[0].astype(jnp.float32), tail_pad)
    )
    value_sum = (
        value_sum
        + jnp.pad(from_lower[1].astype(jnp.float32), edge_pad)
        + jnp.pad(from_upper[1].astype(jnp.float32), tail_pad)
    )
    query_raw_grad, query_gain_part = norm_backward(
        query_raw[0], query_factor, query_gain, query_grad
    )
    key_raw_grad, key_gain_part = norm_backward(key_raw[0], key_factor, key_gain, key_sum)
    gain_sums = mesh_sum(jnp.stack([query_gain_part, key_gain_part]))
    return (
        query_raw_grad[None],
        key_raw_grad[None],
        value_sum.astype(jnp.bfloat16)[None],
        gain_sums,
    )


def solution(mesh):
    placed = (
        P("dp", "ctx", None),
        P("dp", "ctx", None),
        P("dp", "ctx", None),
        P("dp", "ctx", None),
        P(),
        P(),
    )
    return jax.shard_map(
        per_device,
        mesh=mesh,
        in_specs=placed,
        out_specs=(P("dp", "ctx", None), P("dp", "ctx", None), P("dp", "ctx", None), P()),
        check_vma=False,
    )
```

```python
import functools

import jax
import jax.numpy as jnp
from jax import lax
from jax.experimental import pallas as pl
from jax.experimental.pallas import tpu as pltpu
from jax.sharding import PartitionSpec as P

HEADS = 20
HEAD_DIM = 128


NORM_EPS = 1e-06


def padded(block, sides, width):
    for axis, dim in sides:
        count = lax.axis_size(axis)
        forward = [(i, i + 1) for i in range(count - 1)]
        backward = [(target, source) for source, target in forward]
        low = lax.ppermute(
            lax.slice_in_dim(block, block.shape[dim] - width, None, axis=dim), axis, forward
        )
        high = lax.ppermute(lax.slice_in_dim(block, 0, width, axis=dim), axis, backward)
        block = jnp.concatenate([low, block, high], axis=dim)
    return block


AXIS_PARTS = {"ctx": (4, 4, 2), "dp": (8, 3)}
SUM_ORDER = (("dp", 1), ("dp", 0), ("ctx", 0), ("ctx", 1), ("ctx", 2))


def sum_plan():
    plan = []
    for axis, part in SUM_ORDER:
        sizes = AXIS_PARTS[axis]
        stride = 1
        for later in sizes[part + 1:]:
            stride *= later
        size = sizes[part]
        if size & (size - 1):
            plan.append((axis, size, stride, "ring"))
        else:
            d = 1
            while d < size:
                plan.append((axis, size, stride, d))
                d *= 2
    return plan


def moved(index, size, stride, new_coord_fn):
    c = (index // stride) % size
    return index + (new_coord_fn(c) - c) * stride


def step_partners(kind, size, stride, index):
    if kind == "ring":
        return [moved(index, size, stride, lambda c, k=k: (c + k) % size) for k in range(1, size)]
    d = kind
    return [moved(index, size, stride, lambda c: c + d - 2 * d * ((c // d) % 2))]


def sum_kernel(plan, x_ref, o_ref, acc, slots, send_sem, recv_sem):
    here = {"dp": lax.axis_index("dp"), "ctx": lax.axis_index("ctx")}
    steps = []
    for axis, size, stride, kind in plan:
        ids = []
        for other in step_partners(kind, size, stride, here[axis]):
            dev = dict(here)
            dev[axis] = other
            ids.append((dev["dp"], dev["ctx"]))
        steps.append(ids)
    barrier = pltpu.get_barrier_semaphore()
    count = 0
    for ids in steps:
        for dev in ids:
            pl.semaphore_signal(barrier, inc=1, device_id=dev, device_id_type=pl.DeviceIdType.MESH)
            count += 1
    pl.semaphore_wait(barrier, count)
    acc[0] = x_ref[...]
    slot = 0
    for s, ids in enumerate(steps):
        copies = []
        for dev in ids:
            copy = pltpu.make_async_remote_copy(
                src_ref=acc.at[s],
                dst_ref=slots.at[slot],
                send_sem=send_sem.at[slot],
                recv_sem=recv_sem.at[slot],
                device_id=dev,
                device_id_type=pl.DeviceIdType.MESH,
            )
            copy.start()
            copies.append((copy, slot))
            slot += 1
        total = acc[s]
        for copy, used in copies:
            copy.wait()
            total = total + slots[used]
        acc[s + 1] = total
    o_ref[...] = acc[len(steps)]


def mesh_sum(x):
    plan = sum_plan()
    n_slots = sum(len(step_partners(k, s, st, 0)) for _, s, st, k in plan)
    return pl.pallas_call(
        functools.partial(sum_kernel, plan),
        out_shape=jax.ShapeDtypeStruct(x.shape, x.dtype),
        in_specs=[pl.BlockSpec(memory_space=pltpu.VMEM)],
        out_specs=pl.BlockSpec(memory_space=pltpu.VMEM),
        scratch_shapes=[
            pltpu.VMEM((len(plan) + 1,) + x.shape, x.dtype),
            pltpu.VMEM((n_slots,) + x.shape, x.dtype),
            pltpu.SemaphoreType.DMA((n_slots,)),
            pltpu.SemaphoreType.DMA((n_slots,)),
        ],
        compiler_params=pltpu.CompilerParams(collective_id=7, has_side_effects=True),
    )(x)


def shifted(block, axis, distance):
    devices = range(lax.axis_size(axis))
    route = [(i - distance, i) for i in devices if i - distance in devices]
    return lax.ppermute(block, axis, route)


def normalize(raw_rows, gain_row):
    widened = raw_rows.astype(jnp.float32)
    factor = lax.rsqrt(jnp.mean(widened * widened, axis=-1, keepdims=True) + NORM_EPS)
    return ((widened * factor * gain_row).astype(jnp.bfloat16), factor)


def norm_backward(raw_rows, factor, gain_row, upstream):
    widened = raw_rows.astype(jnp.float32)
    scaled = upstream * gain_row
    inner = jnp.mean(widened * scaled, axis=-1, keepdims=True)
    raw_grad = factor * scaled - widened * (factor * factor * factor) * inner
    gain_part = jnp.sum(upstream * widened * factor, axis=0)
    return (raw_grad.astype(jnp.bfloat16), gain_part)


def split_heads(matrix):
    return matrix.reshape(matrix.shape[0], HEADS, HEAD_DIM)


def tile_pass(query_rows, key_rows, value_rows, grad_rows, valid_keys):
    score_scale = HEAD_DIM ** (-0.5)
    query_heads = split_heads(query_rows)
    key_heads = split_heads(key_rows)
    value_heads = split_heads(value_rows)
    grad_heads = split_heads(grad_rows)
    scores = (
        jnp.einsum("qhd,khd->hqk", query_heads, key_heads, preferred_element_type=jnp.float32)
        * score_scale
    )
    scores = jnp.where(valid_keys[None, None, :], scores, -1e30)
    row_max = jnp.max(scores, axis=-1, keepdims=True)
    exponents = jnp.exp(scores - row_max)
    row_sum = jnp.sum(exponents, axis=-1, keepdims=True)
    attn_probs = exponents / row_sum
    probs_half = attn_probs.astype(jnp.bfloat16)
    attn_out = jnp.einsum(
        "hqk,khd->qhd", probs_half, value_heads, preferred_element_type=jnp.float32
    )
    row_delta = jnp.sum(grad_heads.astype(jnp.float32) * attn_out, axis=-1)
    grad_probs = jnp.einsum(
        "qhd,khd->hqk", grad_heads, value_heads, preferred_element_type=jnp.float32
    )
    grad_scores = (attn_probs * (grad_probs - jnp.transpose(row_delta)[:, :, None])).astype(
        jnp.bfloat16
    )
    query_grad = (
        jnp.einsum("hqk,khd->qhd", grad_scores, key_heads, preferred_element_type=jnp.float32)
        * score_scale
    )
    key_terms = (
        jnp.einsum("hqk,qhd->khd", grad_scores, query_heads, preferred_element_type=jnp.float32)
        * score_scale
    ).astype(jnp.bfloat16)
    value_terms = jnp.einsum(
        "hqk,qhd->khd", probs_half, grad_heads, preferred_element_type=jnp.float32
    ).astype(jnp.bfloat16)
    log_total = jnp.transpose((row_max + jnp.log(row_sum))[:, :, 0])
    flat_width = HEADS * HEAD_DIM
    return (
        query_grad.reshape(query_rows.shape[0], flat_width),
        key_terms.reshape(key_rows.shape[0], flat_width),
        value_terms.reshape(key_rows.shape[0], flat_width),
        log_total,
        row_delta,
    )


def per_device(query_raw, key_raw, value_rows, out_grad, query_gain, key_gain):
    tile_rows = query_raw.shape[1]
    margin = tile_rows // 4
    ctx_count = lax.axis_size("ctx")
    position = lax.axis_index("ctx")
    query_norm, query_factor = normalize(query_raw[0], query_gain)
    key_norm, key_factor = normalize(key_raw[0], key_gain)
    own_values = value_rows[0]
    own_grads = out_grad[0]
    key_window = padded(jnp.stack([key_norm, own_values]), (("ctx", 1),), margin)
    slot_ids = jnp.arange(tile_rows + 2 * margin, dtype=jnp.int32)
    valid_keys = jnp.logical_not(
        (slot_ids < margin) & (position == 0)
        | (slot_ids >= margin + tile_rows) & (position == ctx_count - 1)
    )
    query_grad, key_terms, value_terms, log_total, row_delta = tile_pass(
        query_norm, key_window[0], key_window[1], own_grads, valid_keys
    )
    key_sum = key_terms[margin : margin + tile_rows].astype(jnp.float32)
    value_sum = value_terms[margin : margin + tile_rows].astype(jnp.float32)
    edge_pad = ((0, tile_rows - margin), (0, 0))
    tail_pad = ((tile_rows - margin, 0), (0, 0))
    upper_slot = jnp.stack([key_terms[margin + tile_rows :], value_terms[margin + tile_rows :]])
    lower_slot = jnp.stack([key_terms[:margin], value_terms[:margin]])
    from_lower = shifted(upper_slot, "ctx", 1)
    from_upper = shifted(lower_slot, "ctx", -1)
    key_sum = (
        key_sum
        + jnp.pad(from_lower[0].astype(jnp.float32), edge_pad)
        + jnp.pad(from_upper[0].astype(jnp.float32), tail_pad)
    )
    value_sum = (
        value_sum
        + jnp.pad(from_lower[1].astype(jnp.float32), edge_pad)
        + jnp.pad(from_upper[1].astype(jnp.float32), tail_pad)
    )
    query_raw_grad, query_gain_part = norm_backward(
        query_raw[0], query_factor, query_gain, query_grad
    )
    key_raw_grad, key_gain_part = norm_backward(key_raw[0], key_factor, key_gain, key_sum)
    gain_sums = mesh_sum(jnp.stack([query_gain_part, key_gain_part]))
    return (
        query_raw_grad[None],
        key_raw_grad[None],
        value_sum.astype(jnp.bfloat16)[None],
        gain_sums,
    )


def solution(mesh):
    placed = (
        P("dp", "ctx", None),
        P("dp", "ctx", None),
        P("dp", "ctx", None),
        P("dp", "ctx", None),
        P(),
        P(),
    )
    return jax.shard_map(
        per_device,
        mesh=mesh,
        in_specs=placed,
        out_specs=(P("dp", "ctx", None), P("dp", "ctx", None), P("dp", "ctx", None), P()),
        check_vma=False,
    )
```

```python
import functools

import jax
import jax.numpy as jnp
from jax import lax
from jax.experimental import pallas as pl
from jax.experimental.pallas import tpu as pltpu
from jax.sharding import PartitionSpec as P

HEADS = 20
HEAD_DIM = 128


NORM_EPS = 1e-06


def padded(block, sides, width):
    for axis, dim in sides:
        count = lax.axis_size(axis)
        forward = [(i, i + 1) for i in range(count - 1)]
        backward = [(target, source) for source, target in forward]
        low = lax.ppermute(
            lax.slice_in_dim(block, block.shape[dim] - width, None, axis=dim), axis, forward
        )
        high = lax.ppermute(lax.slice_in_dim(block, 0, width, axis=dim), axis, backward)
        block = jnp.concatenate([low, block, high], axis=dim)
    return block


AXIS_PARTS = {"ctx": (4, 4, 2), "dp": (8, 3)}
SUM_ORDER = (("dp", 1), ("dp", 0), ("ctx", 0), ("ctx", 1), ("ctx", 2))


def sum_plan():
    plan = []
    for axis, part in SUM_ORDER:
        sizes = AXIS_PARTS[axis]
        stride = 1
        for later in sizes[part + 1:]:
            stride *= later
        plan.append((axis, sizes[part], stride, "ring"))
    return plan


def moved(index, size, stride, new_coord_fn):
    c = (index // stride) % size
    return index + (new_coord_fn(c) - c) * stride


def step_partners(kind, size, stride, index):
    if kind == "ring":
        return [moved(index, size, stride, lambda c, k=k: (c + k) % size) for k in range(1, size)]
    d = kind
    return [moved(index, size, stride, lambda c: c + d - 2 * d * ((c // d) % 2))]


def sum_kernel(plan, x_ref, o_ref, acc, slots, send_sem, recv_sem):
    here = {"dp": lax.axis_index("dp"), "ctx": lax.axis_index("ctx")}
    steps = []
    for axis, size, stride, kind in plan:
        ids = []
        for other in step_partners(kind, size, stride, here[axis]):
            dev = dict(here)
            dev[axis] = other
            ids.append((dev["dp"], dev["ctx"]))
        steps.append(ids)
    barrier = pltpu.get_barrier_semaphore()
    count = 0
    for ids in steps:
        for dev in ids:
            pl.semaphore_signal(barrier, inc=1, device_id=dev, device_id_type=pl.DeviceIdType.MESH)
            count += 1
    pl.semaphore_wait(barrier, count)
    acc[0] = x_ref[...]
    slot = 0
    for s, ids in enumerate(steps):
        copies = []
        for dev in ids:
            copy = pltpu.make_async_remote_copy(
                src_ref=acc.at[s],
                dst_ref=slots.at[slot],
                send_sem=send_sem.at[slot],
                recv_sem=recv_sem.at[slot],
                device_id=dev,
                device_id_type=pl.DeviceIdType.MESH,
            )
            copy.start()
            copies.append((copy, slot))
            slot += 1
        total = acc[s]
        for copy, used in copies:
            copy.wait()
            total = total + slots[used]
        acc[s + 1] = total
    o_ref[...] = acc[len(steps)]


def mesh_sum(x):
    plan = sum_plan()
    n_slots = sum(len(step_partners(k, s, st, 0)) for _, s, st, k in plan)
    return pl.pallas_call(
        functools.partial(sum_kernel, plan),
        out_shape=jax.ShapeDtypeStruct(x.shape, x.dtype),
        in_specs=[pl.BlockSpec(memory_space=pltpu.VMEM)],
        out_specs=pl.BlockSpec(memory_space=pltpu.VMEM),
        scratch_shapes=[
            pltpu.VMEM((len(plan) + 1,) + x.shape, x.dtype),
            pltpu.VMEM((n_slots,) + x.shape, x.dtype),
            pltpu.SemaphoreType.DMA((n_slots,)),
            pltpu.SemaphoreType.DMA((n_slots,)),
        ],
        compiler_params=pltpu.CompilerParams(collective_id=7, has_side_effects=True),
    )(x)


def shifted(block, axis, distance):
    devices = range(lax.axis_size(axis))
    route = [(i - distance, i) for i in devices if i - distance in devices]
    return lax.ppermute(block, axis, route)


def normalize(raw_rows, gain_row):
    widened = raw_rows.astype(jnp.float32)
    factor = lax.rsqrt(jnp.mean(widened * widened, axis=-1, keepdims=True) + NORM_EPS)
    return ((widened * factor * gain_row).astype(jnp.bfloat16), factor)


def norm_backward(raw_rows, factor, gain_row, upstream):
    widened = raw_rows.astype(jnp.float32)
    scaled = upstream * gain_row
    inner = jnp.mean(widened * scaled, axis=-1, keepdims=True)
    raw_grad = factor * scaled - widened * (factor * factor * factor) * inner
    gain_part = jnp.sum(upstream * widened * factor, axis=0)
    return (raw_grad.astype(jnp.bfloat16), gain_part)


def split_heads(matrix):
    return matrix.reshape(matrix.shape[0], HEADS, HEAD_DIM)


def tile_pass(query_rows, key_rows, value_rows, grad_rows, valid_keys):
    score_scale = HEAD_DIM ** (-0.5)
    query_heads = split_heads(query_rows)
    key_heads = split_heads(key_rows)
    value_heads = split_heads(value_rows)
    grad_heads = split_heads(grad_rows)
    scores = (
        jnp.einsum("qhd,khd->hqk", query_heads, key_heads, preferred_element_type=jnp.float32)
        * score_scale
    )
    scores = jnp.where(valid_keys[None, None, :], scores, -1e30)
    row_max = jnp.max(scores, axis=-1, keepdims=True)
    exponents = jnp.exp(scores - row_max)
    row_sum = jnp.sum(exponents, axis=-1, keepdims=True)
    attn_probs = exponents / row_sum
    probs_half = attn_probs.astype(jnp.bfloat16)
    attn_out = jnp.einsum(
        "hqk,khd->qhd", probs_half, value_heads, preferred_element_type=jnp.float32
    )
    row_delta = jnp.sum(grad_heads.astype(jnp.float32) * attn_out, axis=-1)
    grad_probs = jnp.einsum(
        "qhd,khd->hqk", grad_heads, value_heads, preferred_element_type=jnp.float32
    )
    grad_scores = (attn_probs * (grad_probs - jnp.transpose(row_delta)[:, :, None])).astype(
        jnp.bfloat16
    )
    query_grad = (
        jnp.einsum("hqk,khd->qhd", grad_scores, key_heads, preferred_element_type=jnp.float32)
        * score_scale
    )
    key_terms = (
        jnp.einsum("hqk,qhd->khd", grad_scores, query_heads, preferred_element_type=jnp.float32)
        * score_scale
    ).astype(jnp.bfloat16)
    value_terms = jnp.einsum(
        "hqk,qhd->khd", probs_half, grad_heads, preferred_element_type=jnp.float32
    ).astype(jnp.bfloat16)
    log_total = jnp.transpose((row_max + jnp.log(row_sum))[:, :, 0])
    flat_width = HEADS * HEAD_DIM
    return (
        query_grad.reshape(query_rows.shape[0], flat_width),
        key_terms.reshape(key_rows.shape[0], flat_width),
        value_terms.reshape(key_rows.shape[0], flat_width),
        log_total,
        row_delta,
    )


def per_device(query_raw, key_raw, value_rows, out_grad, query_gain, key_gain):
    tile_rows = query_raw.shape[1]
    margin = tile_rows // 4
    ctx_count = lax.axis_size("ctx")
    position = lax.axis_index("ctx")
    query_norm, query_factor = normalize(query_raw[0], query_gain)
    key_norm, key_factor = normalize(key_raw[0], key_gain)
    own_values = value_rows[0]
    own_grads = out_grad[0]
    key_window = padded(jnp.stack([key_norm, own_values]), (("ctx", 1),), margin)
    slot_ids = jnp.arange(tile_rows + 2 * margin, dtype=jnp.int32)
    valid_keys = jnp.logical_not(
        (slot_ids < margin) & (position == 0)
        | (slot_ids >= margin + tile_rows) & (position == ctx_count - 1)
    )
    query_grad, key_terms, value_terms, log_total, row_delta = tile_pass(
        query_norm, key_window[0], key_window[1], own_grads, valid_keys
    )
    key_sum = key_terms[margin : margin + tile_rows].astype(jnp.float32)
    value_sum = value_terms[margin : margin + tile_rows].astype(jnp.float32)
    edge_pad = ((0, tile_rows - margin), (0, 0))
    tail_pad = ((tile_rows - margin, 0), (0, 0))
    upper_slot = jnp.stack([key_terms[margin + tile_rows :], value_terms[margin + tile_rows :]])
    lower_slot = jnp.stack([key_terms[:margin], value_terms[:margin]])
    from_lower = shifted(upper_slot, "ctx", 1)
    from_upper = shifted(lower_slot, "ctx", -1)
    key_sum = (
        key_sum
        + jnp.pad(from_lower[0].astype(jnp.float32), edge_pad)
        + jnp.pad(from_upper[0].astype(jnp.float32), tail_pad)
    )
    value_sum = (
        value_sum
        + jnp.pad(from_lower[1].astype(jnp.float32), edge_pad)
        + jnp.pad(from_upper[1].astype(jnp.float32), tail_pad)
    )
    query_raw_grad, query_gain_part = norm_backward(
        query_raw[0], query_factor, query_gain, query_grad
    )
    key_raw_grad, key_gain_part = norm_backward(key_raw[0], key_factor, key_gain, key_sum)
    gain_sums = mesh_sum(jnp.stack([query_gain_part, key_gain_part]))
    return (
        query_raw_grad[None],
        key_raw_grad[None],
        value_sum.astype(jnp.bfloat16)[None],
        gain_sums,
    )


def solution(mesh):
    placed = (
        P("dp", "ctx", None),
        P("dp", "ctx", None),
        P("dp", "ctx", None),
        P("dp", "ctx", None),
        P(),
        P(),
    )
    return jax.shard_map(
        per_device,
        mesh=mesh,
        in_specs=placed,
        out_specs=(P("dp", "ctx", None), P("dp", "ctx", None), P("dp", "ctx", None), P()),
        check_vma=False,
    )
```

```python
import functools

import jax
import jax.numpy as jnp
from jax import lax
from jax.experimental import pallas as pl
from jax.experimental.pallas import tpu as pltpu
from jax.sharding import PartitionSpec as P

HEADS = 20
HEAD_DIM = 128


NORM_EPS = 1e-06


def padded(block, sides, width):
    for axis, dim in sides:
        count = lax.axis_size(axis)
        forward = [(i, i + 1) for i in range(count - 1)]
        backward = [(target, source) for source, target in forward]
        low = lax.ppermute(
            lax.slice_in_dim(block, block.shape[dim] - width, None, axis=dim), axis, forward
        )
        high = lax.ppermute(lax.slice_in_dim(block, 0, width, axis=dim), axis, backward)
        block = jnp.concatenate([low, block, high], axis=dim)
    return block


AXIS_PARTS = {"ctx": (4, 4, 2), "dp": (8, 3)}
SUM_ORDER = (("dp", 1), ("dp", 0), ("ctx", 0), ("ctx", 1), ("ctx", 2))


def sum_plan():
    plan = []
    for axis, part in SUM_ORDER:
        sizes = AXIS_PARTS[axis]
        stride = 1
        for later in sizes[part + 1:]:
            stride *= later
        plan.append((axis, sizes[part], stride, "ring"))
    return plan


def moved(index, size, stride, new_coord_fn):
    c = (index // stride) % size
    return index + (new_coord_fn(c) - c) * stride


def step_partners(kind, size, stride, index):
    if kind == "ring":
        return [moved(index, size, stride, lambda c, k=k: (c + k) % size) for k in range(1, size)]
    d = kind
    return [moved(index, size, stride, lambda c: c + d - 2 * d * ((c // d) % 2))]


def sum_kernel(plan, x_ref, o_ref, acc, slots, send_sem, recv_sem):
    here = {"dp": lax.axis_index("dp"), "ctx": lax.axis_index("ctx")}
    steps = []
    for axis, size, stride, kind in plan:
        ids = []
        for other in step_partners(kind, size, stride, here[axis]):
            dev = dict(here)
            dev[axis] = other
            ids.append((dev["dp"], dev["ctx"]))
        steps.append(ids)
    barrier = pltpu.get_barrier_semaphore()
    count = 0
    for ids in steps:
        for dev in ids:
            pl.semaphore_signal(barrier, inc=1, device_id=dev, device_id_type=pl.DeviceIdType.MESH)
            count += 1
    pl.semaphore_wait(barrier, count)
    acc[0] = x_ref[...]
    slot = 0
    for s, ids in enumerate(steps):
        copies = []
        for dev in ids:
            copy = pltpu.make_async_remote_copy(
                src_ref=acc.at[s],
                dst_ref=slots.at[slot],
                send_sem=send_sem.at[slot],
                recv_sem=recv_sem.at[slot],
                device_id=dev,
                device_id_type=pl.DeviceIdType.MESH,
            )
            copy.start()
            copies.append((copy, slot))
            slot += 1
        total = acc[s]
        for copy, used in copies:
            copy.wait()
            total = total + slots[used]
        acc[s + 1] = total
    o_ref[...] = acc[len(steps)]


def mesh_sum(x):
    plan = sum_plan()
    n_slots = sum(len(step_partners(k, s, st, 0)) for _, s, st, k in plan)
    return pl.pallas_call(
        functools.partial(sum_kernel, plan),
        out_shape=jax.ShapeDtypeStruct(x.shape, x.dtype),
        in_specs=[pl.BlockSpec(memory_space=pltpu.VMEM)],
        out_specs=pl.BlockSpec(memory_space=pltpu.VMEM),
        scratch_shapes=[
            pltpu.VMEM((len(plan) + 1,) + x.shape, x.dtype),
            pltpu.VMEM((n_slots,) + x.shape, x.dtype),
            pltpu.SemaphoreType.DMA((n_slots,)),
            pltpu.SemaphoreType.DMA((n_slots,)),
        ],
        compiler_params=pltpu.CompilerParams(collective_id=7, has_side_effects=True),
    )(x)


def shifted(block, axis, distance):
    devices = range(lax.axis_size(axis))
    route = [(i - distance, i) for i in devices if i - distance in devices]
    return lax.ppermute(block, axis, route)


def normalize(raw_rows, gain_row):
    widened = raw_rows.astype(jnp.float32)
    factor = lax.rsqrt(jnp.mean(widened * widened, axis=-1, keepdims=True) + NORM_EPS)
    return ((widened * factor * gain_row).astype(jnp.bfloat16), factor)


def norm_backward(raw_rows, factor, gain_row, upstream):
    widened = raw_rows.astype(jnp.float32)
    scaled = upstream * gain_row
    inner = jnp.mean(widened * scaled, axis=-1, keepdims=True)
    raw_grad = factor * scaled - widened * (factor * factor * factor) * inner
    gain_part = jnp.sum(upstream * widened * factor, axis=0)
    return (raw_grad.astype(jnp.bfloat16), gain_part)


def split_heads(matrix):
    return matrix.reshape(matrix.shape[0], HEADS, HEAD_DIM)


def tile_pass(query_rows, key_rows, value_rows, grad_rows, valid_keys):
    score_scale = HEAD_DIM ** (-0.5)
    query_heads = split_heads(query_rows)
    key_heads = split_heads(key_rows)
    value_heads = split_heads(value_rows)
    grad_heads = split_heads(grad_rows)
    scores = (
        jnp.einsum("qhd,khd->hqk", query_heads, key_heads, preferred_element_type=jnp.float32)
        * score_scale
    )
    scores = jnp.where(valid_keys[None, None, :], scores, -1e30)
    row_max = jnp.max(scores, axis=-1, keepdims=True)
    exponents = jnp.exp(scores - row_max)
    row_sum = jnp.sum(exponents, axis=-1, keepdims=True)
    attn_probs = exponents / row_sum
    probs_half = attn_probs.astype(jnp.bfloat16)
    attn_out = jnp.einsum(
        "hqk,khd->qhd", probs_half, value_heads, preferred_element_type=jnp.float32
    )
    row_delta = jnp.sum(grad_heads.astype(jnp.float32) * attn_out, axis=-1)
    grad_probs = jnp.einsum(
        "qhd,khd->hqk", grad_heads, value_heads, preferred_element_type=jnp.float32
    )
    grad_scores = (attn_probs * (grad_probs - jnp.transpose(row_delta)[:, :, None])).astype(
        jnp.bfloat16
    )
    query_grad = (
        jnp.einsum("hqk,khd->qhd", grad_scores, key_heads, preferred_element_type=jnp.float32)
        * score_scale
    )
    key_terms = (
        jnp.einsum("hqk,qhd->khd", grad_scores, query_heads, preferred_element_type=jnp.float32)
        * score_scale
    ).astype(jnp.bfloat16)
    value_terms = jnp.einsum(
        "hqk,qhd->khd", probs_half, grad_heads, preferred_element_type=jnp.float32
    ).astype(jnp.bfloat16)
    log_total = jnp.transpose((row_max + jnp.log(row_sum))[:, :, 0])
    flat_width = HEADS * HEAD_DIM
    return (
        query_grad.reshape(query_rows.shape[0], flat_width),
        key_terms.reshape(key_rows.shape[0], flat_width),
        value_terms.reshape(key_rows.shape[0], flat_width),
        log_total,
        row_delta,
    )


def per_device(query_raw, key_raw, value_rows, out_grad, query_gain, key_gain):
    tile_rows = query_raw.shape[1]
    margin = tile_rows // 4
    ctx_count = lax.axis_size("ctx")
    position = lax.axis_index("ctx")
    query_norm, query_factor = normalize(query_raw[0], query_gain)
    own_values = value_rows[0]
    own_grads = out_grad[0]
    key_window = padded(jnp.stack([key_raw[0], own_values]), (("ctx", 1),), margin)
    window_keys, window_factor = normalize(key_window[0], key_gain)
    key_factor = window_factor[margin : margin + tile_rows]
    slot_ids = jnp.arange(tile_rows + 2 * margin, dtype=jnp.int32)
    valid_keys = jnp.logical_not(
        (slot_ids < margin) & (position == 0)
        | (slot_ids >= margin + tile_rows) & (position == ctx_count - 1)
    )
    query_grad, key_terms, value_terms, log_total, row_delta = tile_pass(
        query_norm, window_keys, key_window[1], own_grads, valid_keys
    )
    key_sum = key_terms[margin : margin + tile_rows].astype(jnp.float32)
    value_sum = value_terms[margin : margin + tile_rows].astype(jnp.float32)
    edge_pad = ((0, tile_rows - margin), (0, 0))
    tail_pad = ((tile_rows - margin, 0), (0, 0))
    upper_slot = jnp.stack([key_terms[margin + tile_rows :], value_terms[margin + tile_rows :]])
    lower_slot = jnp.stack([key_terms[:margin], value_terms[:margin]])
    from_lower = shifted(upper_slot, "ctx", 1)
    from_upper = shifted(lower_slot, "ctx", -1)
    key_sum = (
        key_sum
        + jnp.pad(from_lower[0].astype(jnp.float32), edge_pad)
        + jnp.pad(from_upper[0].astype(jnp.float32), tail_pad)
    )
    value_sum = (
        value_sum
        + jnp.pad(from_lower[1].astype(jnp.float32), edge_pad)
        + jnp.pad(from_upper[1].astype(jnp.float32), tail_pad)
    )
    query_raw_grad, query_gain_part = norm_backward(
        query_raw[0], query_factor, query_gain, query_grad
    )
    key_raw_grad, key_gain_part = norm_backward(key_raw[0], key_factor, key_gain, key_sum)
    gain_sums = mesh_sum(jnp.stack([query_gain_part, key_gain_part]))
    return (
        query_raw_grad[None],
        key_raw_grad[None],
        value_sum.astype(jnp.bfloat16)[None],
        gain_sums,
    )


def solution(mesh):
    placed = (
        P("dp", "ctx", None),
        P("dp", "ctx", None),
        P("dp", "ctx", None),
        P("dp", "ctx", None),
        P(),
        P(),
    )
    return jax.shard_map(
        per_device,
        mesh=mesh,
        in_specs=placed,
        out_specs=(P("dp", "ctx", None), P("dp", "ctx", None), P("dp", "ctx", None), P()),
        check_vma=False,
    )
```

```python
import functools

import jax
import jax.numpy as jnp
from jax import lax
from jax.experimental import pallas as pl
from jax.experimental.pallas import tpu as pltpu
from jax.sharding import PartitionSpec as P

HEADS = 20
HEAD_DIM = 128


NORM_EPS = 1e-06


def padded(block, sides, width):
    for axis, dim in sides:
        count = lax.axis_size(axis)
        forward = [(i, i + 1) for i in range(count - 1)]
        backward = [(target, source) for source, target in forward]
        low = lax.ppermute(
            lax.slice_in_dim(block, block.shape[dim] - width, None, axis=dim), axis, forward
        )
        high = lax.ppermute(lax.slice_in_dim(block, 0, width, axis=dim), axis, backward)
        block = jnp.concatenate([low, block, high], axis=dim)
    return block


AXIS_PARTS = {"ctx": (4, 4, 2), "dp": (8, 3)}
SUM_ORDER = (("ctx", 2), ("ctx", 1), ("ctx", 0), ("dp", 0), ("dp", 1))


def sum_plan():
    plan = []
    for axis, part in SUM_ORDER:
        sizes = AXIS_PARTS[axis]
        stride = 1
        for later in sizes[part + 1:]:
            stride *= later
        plan.append((axis, sizes[part], stride, "ring"))
    return plan


def moved(index, size, stride, new_coord_fn):
    c = (index // stride) % size
    return index + (new_coord_fn(c) - c) * stride


def step_partners(kind, size, stride, index):
    if kind == "ring":
        return [moved(index, size, stride, lambda c, k=k: (c + k) % size) for k in range(1, size)]
    d = kind
    return [moved(index, size, stride, lambda c: c + d - 2 * d * ((c // d) % 2))]


def sum_kernel(plan, x_ref, o_ref, acc, slots, send_sem, recv_sem):
    here = {"dp": lax.axis_index("dp"), "ctx": lax.axis_index("ctx")}
    steps = []
    for axis, size, stride, kind in plan:
        ids = []
        for other in step_partners(kind, size, stride, here[axis]):
            dev = dict(here)
            dev[axis] = other
            ids.append((dev["dp"], dev["ctx"]))
        steps.append(ids)
    barrier = pltpu.get_barrier_semaphore()
    count = 0
    for ids in steps:
        for dev in ids:
            pl.semaphore_signal(barrier, inc=1, device_id=dev, device_id_type=pl.DeviceIdType.MESH)
            count += 1
    pl.semaphore_wait(barrier, count)
    acc[0] = x_ref[...]
    slot = 0
    for s, ids in enumerate(steps):
        copies = []
        for dev in ids:
            copy = pltpu.make_async_remote_copy(
                src_ref=acc.at[s],
                dst_ref=slots.at[slot],
                send_sem=send_sem.at[slot],
                recv_sem=recv_sem.at[slot],
                device_id=dev,
                device_id_type=pl.DeviceIdType.MESH,
            )
            copy.start()
            copies.append((copy, slot))
            slot += 1
        total = acc[s]
        for copy, used in copies:
            copy.wait()
            total = total + slots[used]
        acc[s + 1] = total
    o_ref[...] = acc[len(steps)]


def mesh_sum(x):
    plan = sum_plan()
    n_slots = sum(len(step_partners(k, s, st, 0)) for _, s, st, k in plan)
    return pl.pallas_call(
        functools.partial(sum_kernel, plan),
        out_shape=jax.ShapeDtypeStruct(x.shape, x.dtype),
        in_specs=[pl.BlockSpec(memory_space=pltpu.VMEM)],
        out_specs=pl.BlockSpec(memory_space=pltpu.VMEM),
        scratch_shapes=[
            pltpu.VMEM((len(plan) + 1,) + x.shape, x.dtype),
            pltpu.VMEM((n_slots,) + x.shape, x.dtype),
            pltpu.SemaphoreType.DMA((n_slots,)),
            pltpu.SemaphoreType.DMA((n_slots,)),
        ],
        compiler_params=pltpu.CompilerParams(collective_id=7, has_side_effects=True),
    )(x)


def shifted(block, axis, distance):
    devices = range(lax.axis_size(axis))
    route = [(i - distance, i) for i in devices if i - distance in devices]
    return lax.ppermute(block, axis, route)


def normalize(raw_rows, gain_row):
    widened = raw_rows.astype(jnp.float32)
    factor = lax.rsqrt(jnp.mean(widened * widened, axis=-1, keepdims=True) + NORM_EPS)
    return ((widened * factor * gain_row).astype(jnp.bfloat16), factor)


def norm_backward(raw_rows, factor, gain_row, upstream):
    widened = raw_rows.astype(jnp.float32)
    scaled = upstream * gain_row
    inner = jnp.mean(widened * scaled, axis=-1, keepdims=True)
    raw_grad = factor * scaled - widened * (factor * factor * factor) * inner
    gain_part = jnp.sum(upstream * widened * factor, axis=0)
    return (raw_grad.astype(jnp.bfloat16), gain_part)


def split_heads(matrix):
    return matrix.reshape(matrix.shape[0], HEADS, HEAD_DIM)


def tile_pass(query_rows, key_rows, value_rows, grad_rows, valid_keys):
    score_scale = HEAD_DIM ** (-0.5)
    query_heads = split_heads(query_rows)
    key_heads = split_heads(key_rows)
    value_heads = split_heads(value_rows)
    grad_heads = split_heads(grad_rows)
    scores = (
        jnp.einsum("qhd,khd->hqk", query_heads, key_heads, preferred_element_type=jnp.float32)
        * score_scale
    )
    scores = jnp.where(valid_keys[None, None, :], scores, -1e30)
    row_max = jnp.max(scores, axis=-1, keepdims=True)
    exponents = jnp.exp(scores - row_max)
    row_sum = jnp.sum(exponents, axis=-1, keepdims=True)
    attn_probs = exponents / row_sum
    probs_half = attn_probs.astype(jnp.bfloat16)
    attn_out = jnp.einsum(
        "hqk,khd->qhd", probs_half, value_heads, preferred_element_type=jnp.float32
    )
    row_delta = jnp.sum(grad_heads.astype(jnp.float32) * attn_out, axis=-1)
    grad_probs = jnp.einsum(
        "qhd,khd->hqk", grad_heads, value_heads, preferred_element_type=jnp.float32
    )
    grad_scores = (attn_probs * (grad_probs - jnp.transpose(row_delta)[:, :, None])).astype(
        jnp.bfloat16
    )
    query_grad = (
        jnp.einsum("hqk,khd->qhd", grad_scores, key_heads, preferred_element_type=jnp.float32)
        * score_scale
    )
    key_terms = (
        jnp.einsum("hqk,qhd->khd", grad_scores, query_heads, preferred_element_type=jnp.float32)
        * score_scale
    ).astype(jnp.bfloat16)
    value_terms = jnp.einsum(
        "hqk,qhd->khd", probs_half, grad_heads, preferred_element_type=jnp.float32
    ).astype(jnp.bfloat16)
    log_total = jnp.transpose((row_max + jnp.log(row_sum))[:, :, 0])
    flat_width = HEADS * HEAD_DIM
    return (
        query_grad.reshape(query_rows.shape[0], flat_width),
        key_terms.reshape(key_rows.shape[0], flat_width),
        value_terms.reshape(key_rows.shape[0], flat_width),
        log_total,
        row_delta,
    )


def per_device(query_raw, key_raw, value_rows, out_grad, query_gain, key_gain):
    tile_rows = query_raw.shape[1]
    margin = tile_rows // 4
    ctx_count = lax.axis_size("ctx")
    position = lax.axis_index("ctx")
    query_norm, query_factor = normalize(query_raw[0], query_gain)
    own_values = value_rows[0]
    own_grads = out_grad[0]
    key_window = padded(jnp.stack([key_raw[0], own_values]), (("ctx", 1),), margin)
    window_keys, window_factor = normalize(key_window[0], key_gain)
    key_factor = window_factor[margin : margin + tile_rows]
    slot_ids = jnp.arange(tile_rows + 2 * margin, dtype=jnp.int32)
    valid_keys = jnp.logical_not(
        (slot_ids < margin) & (position == 0)
        | (slot_ids >= margin + tile_rows) & (position == ctx_count - 1)
    )
    query_grad, key_terms, value_terms, log_total, row_delta = tile_pass(
        query_norm, window_keys, key_window[1], own_grads, valid_keys
    )
    key_sum = key_terms[margin : margin + tile_rows].astype(jnp.float32)
    value_sum = value_terms[margin : margin + tile_rows].astype(jnp.float32)
    edge_pad = ((0, tile_rows - margin), (0, 0))
    tail_pad = ((tile_rows - margin, 0), (0, 0))
    upper_slot = jnp.stack([key_terms[margin + tile_rows :], value_terms[margin + tile_rows :]])
    lower_slot = jnp.stack([key_terms[:margin], value_terms[:margin]])
    from_lower = shifted(upper_slot, "ctx", 1)
    from_upper = shifted(lower_slot, "ctx", -1)
    key_sum = (
        key_sum
        + jnp.pad(from_lower[0].astype(jnp.float32), edge_pad)
        + jnp.pad(from_upper[0].astype(jnp.float32), tail_pad)
    )
    value_sum = (
        value_sum
        + jnp.pad(from_lower[1].astype(jnp.float32), edge_pad)
        + jnp.pad(from_upper[1].astype(jnp.float32), tail_pad)
    )
    query_raw_grad, query_gain_part = norm_backward(
        query_raw[0], query_factor, query_gain, query_grad
    )
    key_raw_grad, key_gain_part = norm_backward(key_raw[0], key_factor, key_gain, key_sum)
    gain_sums = mesh_sum(jnp.stack([query_gain_part, key_gain_part]))
    return (
        query_raw_grad[None],
        key_raw_grad[None],
        value_sum.astype(jnp.bfloat16)[None],
        gain_sums,
    )


def solution(mesh):
    placed = (
        P("dp", "ctx", None),
        P("dp", "ctx", None),
        P("dp", "ctx", None),
        P("dp", "ctx", None),
        P(),
        P(),
    )
    return jax.shard_map(
        per_device,
        mesh=mesh,
        in_specs=placed,
        out_specs=(P("dp", "ctx", None), P("dp", "ctx", None), P("dp", "ctx", None), P()),
        check_vma=False,
    )
```
